512 devices in a mesh: pipe: 8 (over z), expert: 32 (over y, x), dp: 2 (over core).
Axes of the slice: x: 4, y: 8, z: 8, core: 2. Of those that a mesh axis runs over, the one named last changes fastest.
Arguments:
- saved: bfloat16 [1, 8, 8192, 2560], P(None, 'pipe', ('expert', 'dp')), may hold values from -6 to 6
- cotangent: bfloat16 [8192, 2560], P(('expert', 'dp'), 'pipe'), may hold values from -1.1953125 to 1.1953125
- routes: int32 [1, 8, 8192, 1], P(None, 'pipe', ('expert', 'dp')), may hold values from 0 to 7; in each aligned block of 16 rows (0 to 15, 16 to 31, ..., all dimensions but the last counted through in order) at most 2 rows name the same one
- w_gate: bfloat16 [1, 8, 8192, 2560], P(None, 'pipe', 'expert', 'dp'), may hold values from -0.125 to 0.125
- w_up: bfloat16 [1, 8, 8192, 2560], P(None, 'pipe', 'expert', 'dp'), may hold values from -0.125 to 0.125
- w_down: bfloat16 [1, 8, 8192, 2560], P(None, 'pipe', 'expert', 'dp'), may hold values from -0.0625 to 0.0625
Outputs:
- grad_gate: bfloat16 [1, 8, 8192, 2560], P(None, 'pipe', 'expert', 'dp')
- grad_up: bfloat16 [1, 8, 8192, 2560], P(None, 'pipe', 'expert', 'dp')
The draws below stay inside these ranges and needn't reach their ends.
Inputs may be any that keep to these rules, and one draw needn't show every extreme that they name: In each aligned block of 16 rows of routes (one micro-batch of one device, rows taken in order over all leading dimensions) no expert is named more than 2 times.
All inputs are finite; a program needn't handle non-finite values.
Results may differ from the reference program's by a relative error of at most 0.017.
Values may be sent and summed in bfloat16 or wider, within the bound.
No kernel may reach another device: no remote copies, remote signals or barrier semaphores. Data moves between devices by JAX's collectives and lax.ppermute only.
A program may use at most 64 MiB of HBM per device.

```python
import math
import jax
import jax.numpy as jnp
import numpy as np
from jax import lax

D = 2560
HE = 1024
GROUP = 4
V = 1
MICRO = 8
SECTIONS = 8
EXPERTS = 8
HS = 256
HID = 8192
TOK_MB = 16
CAP = 2
TOKENS = 8192
N_DP = 2


def shard_levels(rng, extent, cuts, smallest, high):
    level, own = 1.0, jax.random.fold_in(rng, 6)
    for axis_at, shards_of in cuts:
        heights = jnp.exp(jax.random.uniform(jax.random.fold_in(own, axis_at), (shards_of,), jnp.float32, smallest / len(cuts), high / len(cuts)))
        level = level * jnp.repeat(heights, extent[axis_at] // shards_of).reshape([-1 if axis == axis_at else 1 for axis in range(len(extent))])
    return level


def assign_block(own_key, own, number, rows, count, top, reach, lean):
    sequence = jax.random.permutation(own_key, count)
    packed, ordinary = load_shares(count, rows * top, reach, lean, True), load_shares(count, rows * top, reach, lean, False)
    places = jnp.arange(count)

    def named(sizes, rotation):
        used = int((sizes > 0).sum())
        fixed = max(1, used // 4)
        passed = fixed + (places - fixed + rotation * (used - fixed)) % max(1, count - fixed)
        return jnp.zeros((count,), jnp.int32).at[sequence[jnp.where(places < fixed, places, passed)]].set(jnp.asarray(sizes, jnp.int32))

    sizes = jnp.where(number % 4 == 0, named(packed, number // 4), named(ordinary, number - number // 4 - 1))
    mixed = jax.random.permutation(jax.random.fold_in(own, 3), count)
    giver, sink = mixed[0:count // 2 * 2:2], mixed[1:count // 2 * 2:2]
    margin = jnp.minimum(sizes[giver] - 1, reach - sizes[sink]) // 2
    margin = jnp.where((giver == sequence[0]) | (sink == sequence[0]) | (sizes[sink] == 0), 0, jnp.maximum(margin, 0))
    passed = jax.random.randint(jax.random.fold_in(own, 4), (count // 2,), 0, 1 << 20) % (margin + 1)
    sizes = sizes.at[giver].add(-passed).at[sink].add(passed)
    members = jnp.searchsorted(jnp.cumsum(sizes), jnp.arange(rows * top), side="right").astype(jnp.int32)
    table = members.reshape(top, rows).T
    table = table[jax.random.permutation(jax.random.fold_in(own, 1), rows)]
    rotation = jax.random.randint(jax.random.fold_in(own, 2), (rows, 1), 0, top)
    return jnp.take_along_axis(table, (jnp.arange(top)[None, :] + rotation) % top, axis=1)


def load_shares(count, total, limit, slope, full):
    portions = [(1 << 20) // math.isqrt(grade ** slope) + 1 for grade in range(1, count + 1)]
    largest = limit if full else min(limit, max(-(-total // count), total * portions[0] // sum(portions)))
    least = 1 if total - largest >= count - 1 else 0
    given, spare = [largest] + [least] * (count - 1), total - largest - least * (count - 1)
    while spare > 0:
        movable = [i for i in range(1, count) if given[i] < largest] or [i for i in range(1, count) if given[i] < limit]
        whole, budget = sum([portions[i] for i in movable]), spare
        for i in movable:
            more = min(limit - given[i], max(1, budget * portions[i] // whole), spare)
            given[i] = given[i] + more
            spare = spare - more
    return np.array(given)


def gaussian(own_key, extent, deviation, reach, pieces=(), held_as=jnp.bfloat16):
    gain = shard_levels(own_key, extent, pieces, -0.22, 0.18) if pieces else 1.0
    drawn = jax.random.normal(own_key, extent, jnp.float32) * deviation * gain
    return jnp.minimum(jnp.maximum(drawn, -reach), reach).astype(held_as)


def setup_inputs(seed: int = 0) -> dict:
    keys = jax.random.split(jax.random.key(seed), 7)
    saved = gaussian(keys[0], (V, SECTIONS, TOKENS, D), 1.0, 6.0, ((1, 8), (2, 64)))
    cotangent = gaussian(keys[1], (TOKENS, D), 0.2, 1.1953125, ((0, 64), (1, 8)))
    routes_keys = jax.random.split(jax.random.fold_in(keys[2], 1), V * SECTIONS * TOKENS // TOK_MB)
    routes_turns = jax.random.permutation(jax.random.fold_in(keys[2], 3), V * SECTIONS * TOKENS // TOK_MB)
    routes = jax.vmap(lambda own, number: assign_block(jax.random.fold_in(keys[2], 2), own, number, TOK_MB, EXPERTS, 1, CAP, 0))(routes_keys, routes_turns).reshape((V, SECTIONS, TOKENS, 1))
    w_gate = gaussian(keys[3], (V, SECTIONS, HID, D), D ** -0.5, 0.125, ((1, 8), (2, 32), (3, 2)))
    w_up = gaussian(keys[4], (V, SECTIONS, HID, D), D ** -0.5, 0.125, ((1, 8), (2, 32), (3, 2)))
    w_down = gaussian(keys[5], (V, SECTIONS, HID, D), (8 * HE) ** -0.5, 0.0625, ((1, 8), (2, 32), (3, 2)))
    return {"saved": saved, "cotangent": cotangent, "routes": routes, "w_gate": w_gate, "w_up": w_up, "w_down": w_down}


epsilon = 1e-06

def slot_numbers(route_ids):
    onehot = (route_ids[:, None] == jnp.arange(EXPERTS, dtype=jnp.int32)[None, :]).astype(jnp.int32)
    blocked = onehot.reshape(TOKENS // TOK_MB, TOK_MB, EXPERTS)
    ranking = lax.optimization_barrier(jnp.sum((jnp.cumsum(blocked, axis=1) - blocked) * blocked, axis=2)).reshape(TOKENS)
    block_ids = jnp.arange(TOKENS, dtype=jnp.int32) // TOK_MB
    return (block_ids * CAP + ranking).astype(jnp.int32)

def rounded_sum(total, term):
    kept = lax.optimization_barrier(term.astype(jnp.bfloat16))
    return total + kept.astype(jnp.float32)

def expert_backward(operands):
    unit_rows, grad_rows, gate_w, up_w, down_w = operands
    slot_total = unit_rows.shape[0]
    gate = jnp.dot(unit_rows, gate_w.T, preferred_element_type=jnp.float32)
    up = jnp.dot(unit_rows, up_w.T, preferred_element_type=jnp.float32)
    hidden_grad = jnp.dot(grad_rows, down_w.T, preferred_element_type=jnp.float32)
    sigmoid_gate = jax.nn.sigmoid(gate)
    gate_grad = (hidden_grad * up * sigmoid_gate * (1.0 + gate * (1.0 - sigmoid_gate))).astype(jnp.bfloat16)
    up_grad = (hidden_grad * gate * sigmoid_gate).astype(jnp.bfloat16)
    unit_grad = jnp.zeros((slot_total, D), jnp.float32)
    for slab_index in range(GROUP):
        first = slab_index * HS
        term = jnp.dot(gate_grad[:, first:first + HS], gate_w[first:first + HS], preferred_element_type=jnp.float32)
        term = term + jnp.dot(up_grad[:, first:first + HS], up_w[first:first + HS], preferred_element_type=jnp.float32)
        unit_grad = rounded_sum(unit_grad, term)
    halves = jnp.arange(slot_total, dtype=jnp.int32) // CAP // MICRO % N_DP
    gate_total = jnp.zeros((HE, D), jnp.float32)
    up_total = jnp.zeros((HE, D), jnp.float32)
    for half_index in range(N_DP):
        keep = (halves == half_index)[:, None]
        gate_kept = jnp.where(keep, gate_grad, jnp.zeros_like(gate_grad))
        up_kept = jnp.where(keep, up_grad, jnp.zeros_like(up_grad))
        gate_total = rounded_sum(gate_total, jnp.dot(gate_kept.T, unit_rows, preferred_element_type=jnp.float32))
        up_total = rounded_sum(up_total, jnp.dot(up_kept.T, unit_rows, preferred_element_type=jnp.float32))
    return (unit_grad, gate_total.astype(jnp.bfloat16), up_total.astype(jnp.bfloat16))

def layer_backward(inputs, grad, route_ids, gate_all, up_all, down_all):
    inputs_f = inputs.astype(jnp.float32)
    norm_scale = lax.rsqrt(lax.optimization_barrier(jnp.mean(inputs_f * inputs_f, axis=1, keepdims=True)) + epsilon)
    unit_f = inputs_f * norm_scale
    unit = unit_f.astype(jnp.bfloat16)
    slot_ids = slot_numbers(route_ids)
    slot_total = TOKENS // TOK_MB * CAP
    unit_buffer = jnp.zeros((EXPERTS, slot_total, D), jnp.bfloat16).at[route_ids, slot_ids].set(unit)
    grad_buffer = jnp.zeros((EXPERTS, slot_total, D), jnp.bfloat16).at[route_ids, slot_ids].set(grad)
    unit_grads, gate_grads, up_grads = lax.map(expert_backward, (unit_buffer, grad_buffer, gate_all.reshape(EXPERTS, HE, D), up_all.reshape(EXPERTS, HE, D), down_all.reshape(EXPERTS, HE, D)))
    unit_grad = unit_grads[route_ids, slot_ids]
    norm_grad = norm_scale * (unit_grad - unit_f * lax.optimization_barrier(jnp.mean(unit_grad * unit_f, axis=1, keepdims=True)))
    new_grad = (grad.astype(jnp.float32) + norm_grad).astype(jnp.bfloat16)
    return (new_grad, gate_grads.reshape(HID, D), up_grads.reshape(HID, D))

def reference(saved, cotangent, routes, w_gate, w_up, w_down):
    grad = cotangent
    gate_table = [[None] * SECTIONS for stretch_index in range(V)]
    up_table = [[None] * SECTIONS for stretch_index in range(V)]
    for layer_index in range(V * SECTIONS - 1, -1, -1):
        stretch_index = layer_index // SECTIONS
        section_index = layer_index % SECTIONS
        grad, gate_out, up_out = layer_backward(saved[stretch_index, section_index], grad, routes[stretch_index, section_index, :, 0], w_gate[stretch_index, section_index], w_up[stretch_index, section_index], w_down[stretch_index, section_index])
        gate_table[stretch_index][section_index] = gate_out
        up_table[stretch_index][section_index] = up_out
    grad_gate = jnp.stack([jnp.stack(row_list) for row_list in gate_table])
    grad_up = jnp.stack([jnp.stack(row_list) for row_list in up_table])
    return (grad_gate, grad_up)
```

```python
import jax
import jax.numpy as jnp
from jax import lax
from jax.sharding import PartitionSpec as P

GROUP = 4
MICRO = 8
EPS = 1e-06
F32 = jnp.float32
BF16 = jnp.bfloat16


def dot_t(a, b):
    return lax.dot_general(a, b, (((1,), (1,)), ((), ())), preferred_element_type=F32)


def dot_n(a, b):
    return lax.dot_general(a, b, (((1,), (0,)), ((), ())), preferred_element_type=F32)


def placing_of(route_ids, experts, capacity):
    onehot = (route_ids[..., None] == jnp.arange(experts, dtype=jnp.int32)).astype(jnp.int32)
    ranking = jnp.sum((jnp.cumsum(onehot, axis=1) - onehot) * onehot, axis=2)
    slot_ids = route_ids * capacity + ranking
    positions = jnp.arange(experts * capacity, dtype=jnp.int32)[:, None]
    return (slot_ids[:, None, :] == positions).astype(BF16)


def shards(saved, cotangent, routes, w_gate, w_up, w_down):
    layers = lax.axis_size("pipe")
    width = lax.axis_size("expert")
    dp_index = lax.axis_index("dp")
    experts = width // GROUP
    feat = saved.shape[3]
    half = w_gate.shape[3]
    hidden = w_gate.shape[2]
    tok = saved.shape[2] // MICRO
    cap = tok // experts
    rows_n = width * cap

    wd_all = lax.all_gather(w_down[0, 0], ("pipe", "dp"), axis=0).reshape(layers, 2, hidden, half)
    wg_all = lax.all_gather(w_gate[0, 0], ("pipe", "dp"), axis=0).reshape(layers, 2, hidden, half)
    wu_all = lax.all_gather(w_up[0, 0], ("pipe", "dp"), axis=0).reshape(layers, 2, hidden, half)

    place = placing_of(routes[0, 0, :, 0].reshape(MICRO, tok), experts, cap)
    x = saved[0, 0].reshape(MICRO, tok, feat)
    x_slot = jnp.einsum("mst,mtd->msd", place, x, preferred_element_type=F32)
    scale = lax.rsqrt(jnp.mean(x_slot * x_slot, axis=2, keepdims=True) + EPS)
    unit = (x_slot * scale).astype(BF16)
    send = jnp.broadcast_to(
        unit.reshape(MICRO, experts, 1, cap, feat), (MICRO, experts, GROUP, cap, feat)
    ).reshape(MICRO, width, cap, feat)
    unit_rows = lax.all_to_all(send, "expert", split_axis=1, concat_axis=1, tiled=True)
    unit_rows = unit_rows.reshape(MICRO * rows_n, feat)

    extra = jnp.zeros((MICRO, tok, 128 - tok), BF16)
    cot = cotangent.reshape(MICRO, tok, cotangent.shape[1])
    pack = jnp.concatenate([x_slot.astype(BF16), place, extra, cot], axis=2)
    pack = lax.all_to_all(pack, "pipe", split_axis=0, concat_axis=0, tiled=True)
    x_all = pack[:, :, :feat]
    place_all = pack[:, :, feat : feat + tok]
    grad = jnp.transpose(pack[:, :, feat + 128 :], (1, 0, 2)).reshape(tok, feat)

    swap = [(0, 1), (1, 0)]
    wg_other = lax.ppermute(w_gate[0, 0], "dp", swap)
    wu_other = lax.ppermute(w_up[0, 0], "dp", swap)
    own = lax.dynamic_slice_in_dim(unit_rows, dp_index * half, half, 1)
    other = lax.dynamic_slice_in_dim(unit_rows, (1 - dp_index) * half, half, 1)
    gate = dot_t(own, w_gate[0, 0]) + dot_t(other, wg_other)
    up = dot_t(own, w_up[0, 0]) + dot_t(other, wu_other)
    sig = jax.nn.sigmoid(gate)
    fac = jnp.concatenate([up * sig * (1.0 + gate * (1.0 - sig)), gate * sig], axis=1).astype(BF16)
    fac = lax.all_to_all(
        fac.reshape(MICRO, rows_n, 2 * hidden), "pipe", split_axis=0, concat_axis=0, tiled=True
    )

    kept = [None] * layers
    grad = dot_n(place_all[layers - 1], grad).astype(BF16)
    for layer in range(layers - 1, -1, -1):
        send = jnp.broadcast_to(
            grad.reshape(experts, 1, cap, feat), (experts, GROUP, cap, feat)
        ).reshape(width, cap, feat)
        rows = lax.all_to_all(send, "expert", split_axis=0, concat_axis=0, tiled=True)
        rows = rows.reshape(rows_n, feat)
        hidden_grad = dot_t(rows[:, :half], wd_all[layer, 0]) + dot_t(
            rows[:, half:], wd_all[layer, 1]
        )
        both = (jnp.concatenate([hidden_grad, hidden_grad], axis=1) * fac[layer].astype(F32)).astype(
            BF16
        )
        kept[layer] = both
        if layer == 0:
            break
        gate_grad = both[:, :hidden]
        up_grad = both[:, hidden:]
        partial = jnp.concatenate(
            [
                dot_n(gate_grad, wg_all[layer, c]) + dot_n(up_grad, wu_all[layer, c])
                for c in range(2)
            ],
            axis=1,
        ).astype(BF16)
        back = lax.all_to_all(
            partial.reshape(width, cap, feat), "expert", split_axis=0, concat_axis=0, tiled=True
        )
        unit_grad = back.reshape(experts, GROUP, cap, feat).astype(F32).sum(axis=1).reshape(tok, feat)
        xl = x_all[layer].astype(F32)
        sc = lax.rsqrt(jnp.mean(xl * xl, axis=1, keepdims=True) + EPS)
        x_hat = xl * sc
        norm_grad = sc * (unit_grad - x_hat * jnp.mean(unit_grad * x_hat, axis=1, keepdims=True))
        grad = (grad.astype(F32) + norm_grad).astype(BF16)
        move = dot_t(place_all[layer - 1], place_all[layer]).astype(BF16)
        grad = dot_n(move, grad).astype(BF16)

    grads = lax.all_to_all(jnp.stack(kept), "pipe", split_axis=0, concat_axis=0, tiled=True)
    grads = grads.reshape(MICRO * rows_n, 2 * hidden)
    own = lax.dynamic_slice_in_dim(unit_rows, dp_index * half, half, 1)
    other = lax.dynamic_slice_in_dim(unit_rows, (1 - dp_index) * half, half, 1)
    outer = lambda r: lax.dot_general(
        grads, r, (((0,), (0,)), ((), ())), preferred_element_type=F32
    ).astype(BF16)
    got = lax.ppermute(outer(other), "dp", swap)
    total = (outer(own).astype(F32) + got.astype(F32)).astype(BF16)
    return total[None, None, :hidden], total[None, None, hidden:]


def solution(mesh):
    in_specs = (
        P(None, "pipe", ("expert", "dp"), None),
        P(("expert", "dp"), "pipe"),
        P(None, "pipe", ("expert", "dp"), None),
        P(None, "pipe", "expert", "dp"),
        P(None, "pipe", "expert", "dp"),
        P(None, "pipe", "expert", "dp"),
    )
    out_specs = (P(None, "pipe", "expert", "dp"), P(None, "pipe", "expert", "dp"))
    return jax.shard_map(shards, mesh=mesh, in_specs=in_specs, out_specs=out_specs, check_vma=False)
```

```python
import jax
import jax.numpy as jnp
from jax import lax
from jax.experimental import pallas as pl
from jax.experimental.pallas import tpu as pltpu
from jax.sharding import PartitionSpec as P

GROUP = 4
MICRO = 8
PARTS = 4
EPS = 1e-06
F32 = jnp.float32
BF16 = jnp.bfloat16
SETS = ((7, 6), (5, 4, 3), (2, 1, 0))


def dot_t(a, b):
    return lax.dot_general(a, b, (((1,), (1,)), ((), ())), preferred_element_type=F32)


def dot_n(a, b):
    return lax.dot_general(a, b, (((1,), (0,)), ((), ())), preferred_element_type=F32)


def placing_of(route_ids, experts, capacity):
    onehot = (route_ids[..., None] == jnp.arange(experts, dtype=jnp.int32)).astype(jnp.int32)
    ranking = jnp.sum((jnp.cumsum(onehot, axis=1) - onehot) * onehot, axis=2)
    slot_ids = route_ids * capacity + ranking
    positions = jnp.arange(experts * capacity, dtype=jnp.int32)[:, None]
    return (slot_ids[:, None, :] == positions).astype(BF16)


def expert_call(layer, where, last, rows, weights, fac, kept):
    n_in, lanes = rows.shape
    rows_n = n_in // PARTS
    chunks, _, _, _, rows_c, half = weights.shape
    hidden = chunks * rows_c
    per_half = half // lanes
    mats = 1 if last else 3

    def body(rows_ref, w_ref, fac_ref, _, *refs):
        kept_ref = refs[0]
        outs = refs[1:]
        if last:
            w_vm, stage, sem = outs
        else:
            out_ref, w_vm, stage, sem = outs
        copies = [
            [
                pltpu.make_async_copy(w_ref.at[:, c, where, m], w_vm.at[m, c], sem.at[m, c])
                for c in range(2)
            ]
            for m in range(mats)
        ]
        for pair in copies:
            for copy in pair:
                copy.start()
        blocks = lanes // 128
        for b in range(blocks):
            stage[b] = rows_ref[:, b * 128 : (b + 1) * 128].astype(F32)
        hidden_grad = jnp.zeros((rows_n, hidden), F32)
        for c in range(2):
            copies[0][c].wait()
            for j in range(per_half):
                k = c * per_half + j
                part = jnp.concatenate(
                    [stage[b, pl.ds(k, rows_n, stride=PARTS), :] for b in range(blocks)], axis=1
                ).astype(BF16)
                w = w_vm[0, c, :, :, j * lanes : (j + 1) * lanes].reshape(hidden, lanes)
                hidden_grad = hidden_grad + dot_t(part, w)
        f = fac_ref[0].astype(F32)
        gate_grad = (hidden_grad * f[:, :hidden]).astype(BF16)
        up_grad = (hidden_grad * f[:, hidden:]).astype(BF16)
        kept_ref[0, :, :hidden] = gate_grad
        kept_ref[0, :, hidden:] = up_grad
        if last:
            return
        for c in range(2):
            copies[1][c].wait()
            copies[2][c].wait()
            for j in range(per_half):
                k = c * per_half + j
                g = w_vm[1, c, :, :, j * lanes : (j + 1) * lanes].reshape(hidden, lanes)
                u = w_vm[2, c, :, :, j * lanes : (j + 1) * lanes].reshape(hidden, lanes)
                part = dot_n(gate_grad, g) + dot_n(up_grad, u)
                for b in range(blocks):
                    stage[b, pl.ds(k, rows_n, stride=PARTS), :] = part[:, b * 128 : (b + 1) * 128]
        for b in range(blocks):
            out_ref[:, b * 128 : (b + 1) * 128] = stage[b].astype(BF16)

    block = pl.BlockSpec((1, rows_n, 2 * hidden), lambda i: (layer, 0, 0))
    whole = pl.BlockSpec((n_in, lanes), lambda i: (0, 0))
    out_shape = [jax.ShapeDtypeStruct(kept.shape, BF16)]
    out_specs = [block]
    if not last:
        out_shape.append(jax.ShapeDtypeStruct((n_in, lanes), BF16))
        out_specs.append(whole)
    return pl.pallas_call(
        body,
        grid=(1,),
        in_specs=[
            whole,
            pl.BlockSpec(memory_space=pl.ANY),
            block,
            pl.BlockSpec(memory_space=pl.ANY),
        ],
        out_specs=out_specs,
        out_shape=out_shape,
        scratch_shapes=[
            pltpu.VMEM((mats, 2, chunks, rows_c, half), BF16),
            pltpu.VMEM((lanes // 128, n_in, 128), F32),
            pltpu.SemaphoreType.DMA((3, 2)),
        ],
        input_output_aliases={3: 0},
        compiler_params=pltpu.CompilerParams(vmem_limit_bytes=24 * 1024 * 1024),
        cost_estimate=pl.CostEstimate(
            flops=6 * rows_n * hidden * 2 * half, bytes_accessed=mats * 4 * hidden * half, transcendentals=0
        ),
        name="expert",
    )(rows, weights, fac, kept)


def spread(send_ref, g, experts):
    size = g.shape[0] // experts
    for e in range(experts):
        piece = g[e * size : (e + 1) * size].astype(BF16)
        for q in range(GROUP):
            send_ref[e * GROUP + q] = piece


def home_call(layer, experts, back, grad, x, move):
    n_in, lanes = back.shape
    slots = n_in // GROUP
    size = slots // experts
    features = PARTS * lanes

    def body(back_ref, grad_ref, x_ref, move_ref, out_ref, send_ref):
        total = back_ref[...].astype(F32).reshape(experts, GROUP, size, lanes).sum(axis=1)
        total = total.reshape(slots, lanes)
        xf = x_ref[0].astype(F32)
        square = jnp.sum(xf * xf, axis=1, keepdims=True)
        cross = jnp.sum(total * xf, axis=1, keepdims=True)
        row = lax.broadcasted_iota(jnp.int32, (slots, slots), 0) // PARTS
        col = lax.broadcasted_iota(jnp.int32, (slots, slots), 1) // PARTS
        same = (row == col).astype(F32) * (1.0 / features)
        lane = lax.broadcasted_iota(jnp.int32, (slots, 128), 1)
        sums = jnp.where(lane < 64, square, cross)
        means = lax.dot_general(
            same, sums, (((1,), (0,)), ((), ())),
            precision=lax.Precision.HIGHEST, preferred_element_type=F32,
        )
        scale = lax.rsqrt(means[:, :1] + EPS)
        mean = scale * means[:, 64:65]
        grad_new = grad_ref[...].astype(F32) + scale * (total - (xf * scale) * mean)
        moved = dot_n(move_ref[0], grad_new.astype(BF16))
        out_ref[...] = moved.astype(BF16)
        spread(send_ref, moved, experts)

    return pl.pallas_call(
        body,
        grid=(1,),
        in_specs=[
            pl.BlockSpec((n_in, lanes), lambda i: (0, 0)),
            pl.BlockSpec((slots, lanes), lambda i: (0, 0)),
            pl.BlockSpec((1, slots, lanes), lambda i: (layer, 0, 0)),
            pl.BlockSpec((1, slots, slots), lambda i: (layer, 0, 0)),
        ],
        out_specs=[
            pl.BlockSpec((slots, lanes), lambda i: (0, 0)),
            pl.BlockSpec((experts * GROUP, size, lanes), lambda i: (0, 0, 0)),
        ],
        out_shape=[
            jax.ShapeDtypeStruct((slots, lanes), BF16),
            jax.ShapeDtypeStruct((experts * GROUP, size, lanes), BF16),
        ],
        cost_estimate=pl.CostEstimate(flops=10 * n_in * lanes, bytes_accessed=4 * n_in * lanes, transcendentals=0),
        name="home",
    )(back, grad, x, move)


def shards(saved, cotangent, routes, w_gate, w_up, w_down):
    layers = lax.axis_size("pipe")
    width = lax.axis_size("expert")
    dp_index = lax.axis_index("dp")
    experts = width // GROUP
    feat = saved.shape[3]
    half = w_gate.shape[3]
    hidden = w_gate.shape[2]
    tok = saved.shape[2] // MICRO
    cap = tok // experts
    rows_n = width * cap
    lanes = feat // PARTS
    slots = tok * PARTS
    size = cap * PARTS

    place = placing_of(routes[0, 0, :, 0].reshape(MICRO, tok), experts, cap)
    x = saved[0, 0].reshape(MICRO, tok, feat)
    x_slot = jnp.einsum("mst,mtd->msd", place, x, preferred_element_type=F32)

    thin = cotangent.shape[1] // PARTS
    extra = jnp.concatenate(
        [
            jnp.repeat(place, PARTS, axis=1),
            cotangent.reshape(MICRO, slots, thin),
            jnp.zeros((MICRO, slots, 128 - tok - thin), BF16),
        ],
        axis=2,
    )
    pack = jnp.concatenate([x_slot.astype(BF16).reshape(MICRO, slots, lanes), extra], axis=2)
    pack = lax.all_to_all(pack, "pipe", split_axis=0, concat_axis=0, tiled=True)
    x_all = pack[:, :, :lanes]
    place_all = pack[:, :, lanes : lanes + tok]
    grad = pack[:, :, lanes + tok : lanes + tok + thin].reshape(layers, tok, PARTS * thin)
    grad = jnp.transpose(grad, (1, 0, 2)).reshape(tok, feat)
    grad = dot_n(place_all[layers - 1, ::PARTS], grad).astype(BF16).reshape(slots, lanes)
    quarter = jnp.arange(slots, dtype=jnp.int32) % PARTS
    move = jnp.einsum("lat,lbt->lab", jnp.roll(place_all, 1, axis=0), place_all, preferred_element_type=F32)
    move = jnp.where(quarter[:, None] == quarter[None, :], move, 0.0).astype(BF16)

    cut = jnp.stack([w_down[0, 0], w_gate[0, 0], w_up[0, 0]]).reshape(3, layers, hidden // layers, half)
    cut = lax.all_to_all(cut, "pipe", split_axis=1, concat_axis=1, tiled=True)
    weights = {}
    for members in SETS:
        low = min(members)
        got = lax.all_gather(
            jnp.transpose(cut[:, low : low + len(members)], (1, 0, 2, 3)), ("pipe", "dp"), axis=0
        ).reshape(layers, 2, len(members), 3, hidden // layers, half)
        for layer in members:
            weights[layer] = (got, layer - low)

    scale = lax.rsqrt(jnp.mean(x_slot * x_slot, axis=2, keepdims=True) + EPS)
    unit = (x_slot * scale).astype(BF16)
    send = jnp.broadcast_to(
        unit.reshape(MICRO, experts, 1, cap, feat), (MICRO, experts, GROUP, cap, feat)
    ).reshape(MICRO, width, cap, feat)
    unit_rows = lax.all_to_all(send, "expert", split_axis=1, concat_axis=1, tiled=True)
    unit_rows = unit_rows.reshape(MICRO * rows_n, feat)
    swap = [(0, 1), (1, 0)]
    wg_other = lax.ppermute(w_gate[0, 0], "dp", swap)
    wu_other = lax.ppermute(w_up[0, 0], "dp", swap)
    own = lax.dynamic_slice_in_dim(unit_rows, dp_index * half, half, 1)
    other = lax.dynamic_slice_in_dim(unit_rows, (1 - dp_index) * half, half, 1)
    gate = dot_t(own, w_gate[0, 0]) + dot_t(other, wg_other)
    up = dot_t(own, w_up[0, 0]) + dot_t(other, wu_other)
    sig = jax.nn.sigmoid(gate)
    fac = jnp.concatenate([up * sig * (1.0 + gate * (1.0 - sig)), gate * sig], axis=1).astype(BF16)
    fac = lax.all_to_all(
        fac.reshape(MICRO, rows_n, 2 * hidden), "pipe", split_axis=0, concat_axis=0, tiled=True
    )

    def exchange(block):
        block = block.reshape(width, size, lanes)
        block = lax.all_to_all(block, "expert", split_axis=0, concat_axis=0, tiled=True)
        return block.reshape(width * size, lanes)

    kept = jnp.zeros((layers, rows_n, 2 * hidden), BF16)
    send = jnp.broadcast_to(
        grad.reshape(experts, 1, size, lanes), (experts, GROUP, size, lanes)
    ).reshape(width, size, lanes)
    for layer in range(layers - 1, -1, -1):
        rows = exchange(send)
        got, where = weights[layer]
        if layer == 0:
            (kept,) = expert_call(layer, where, True, rows, got, fac, kept)
            break
        kept, partial = expert_call(layer, where, False, rows, got, fac, kept)
        grad, send = home_call(layer, experts, exchange(partial), grad, x_all, move)

    grads = lax.all_to_all(kept, "pipe", split_axis=0, concat_axis=0, tiled=True)
    grads = grads.reshape(MICRO * rows_n, 2 * hidden)

    def outer(rows):
        return lax.dot_general(
            grads, rows, (((0,), (0,)), ((), ())), preferred_element_type=F32
        ).astype(BF16)

    got = lax.ppermute(outer(other), "dp", swap)
    total = (outer(own).astype(F32) + got.astype(F32)).astype(BF16)
    return total[None, None, :hidden], total[None, None, hidden:]


def solution(mesh):
    in_specs = (
        P(None, "pipe", ("expert", "dp"), None),
        P(("expert", "dp"), "pipe"),
        P(None, "pipe", ("expert", "dp"), None),
        P(None, "pipe", "expert", "dp"),
        P(None, "pipe", "expert", "dp"),
        P(None, "pipe", "expert", "dp"),
    )
    out_specs = (P(None, "pipe", "expert", "dp"), P(None, "pipe", "expert", "dp"))
    return jax.shard_map(shards, mesh=mesh, in_specs=in_specs, out_specs=out_specs, check_vma=False)
```

```python
import jax
import jax.numpy as jnp
from jax import lax
from jax.experimental import pallas as pl
from jax.experimental.pallas import tpu as pltpu
from jax.sharding import PartitionSpec as P


GROUP = 4
MICRO = 8
PARTS = 4
EPS = 1e-06
F32 = jnp.float32
BF16 = jnp.bfloat16
SETS = ((7, 6), (5, 4, 3), (2, 1, 0))


def dot_t(a, b):
    return lax.dot_general(a, b, (((1,), (1,)), ((), ())), preferred_element_type=F32)


def dot_n(a, b):
    return lax.dot_general(a, b, (((1,), (0,)), ((), ())), preferred_element_type=F32)


def placing_of(route_ids, experts, capacity):
    onehot = (route_ids[..., None] == jnp.arange(experts, dtype=jnp.int32)).astype(jnp.int32)
    ranking = jnp.sum((jnp.cumsum(onehot, axis=1) - onehot) * onehot, axis=2)
    slot_ids = route_ids * capacity + ranking
    positions = jnp.arange(experts * capacity, dtype=jnp.int32)[:, None]
    return (slot_ids[:, None, :] == positions).astype(BF16)


def expert_call(layer, where, last, rows, weights, fac, kept):
    n_in, lanes = rows.shape
    rows_n = n_in // PARTS
    chunks, _, _, _, rows_c, half = weights.shape
    hidden = chunks * rows_c
    per_half = half // lanes
    mats = 1 if last else 3

    def body(rows_ref, w_ref, fac_ref, _, *refs):
        kept_ref = refs[0]
        outs = refs[1:]
        if last:
            w_vm, stage, sem = outs
        else:
            out_ref, w_vm, stage, sem = outs
        copies = [
            [
                pltpu.make_async_copy(w_ref.at[:, c, where, m], w_vm.at[m, c], sem.at[m, c])
                for c in range(2)
            ]
            for m in range(mats)
        ]
        for pair in copies:
            for copy in pair:
                copy.start()
        blocks = lanes // 128
        for b in range(blocks):
            stage[b] = rows_ref[:, b * 128 : (b + 1) * 128].astype(F32)
        hidden_grad = jnp.zeros((rows_n, hidden), F32)
        for c in range(2):
            copies[0][c].wait()
            for j in range(per_half):
                k = c * per_half + j
                part = jnp.concatenate(
                    [stage[b, pl.ds(k, rows_n, stride=PARTS), :] for b in range(blocks)], axis=1
                ).astype(BF16)
                w = w_vm[0, c, :, :, j * lanes : (j + 1) * lanes].reshape(hidden, lanes)
                hidden_grad = hidden_grad + dot_t(part, w)
        f = fac_ref[0].astype(F32)
        gate_grad = (hidden_grad * f[:, :hidden]).astype(BF16)
        up_grad = (hidden_grad * f[:, hidden:]).astype(BF16)
        kept_ref[0, :, :hidden] = gate_grad
        kept_ref[0, :, hidden:] = up_grad
        if last:
            return
        for c in range(2):
            copies[1][c].wait()
            copies[2][c].wait()
            for j in range(per_half):
                k = c * per_half + j
                g = w_vm[1, c, :, :, j * lanes : (j + 1) * lanes].reshape(hidden, lanes)
                u = w_vm[2, c, :, :, j * lanes : (j + 1) * lanes].reshape(hidden, lanes)
                part = dot_n(gate_grad, g) + dot_n(up_grad, u)
                for b in range(blocks):
                    stage[b, pl.ds(k, rows_n, stride=PARTS), :] = part[:, b * 128 : (b + 1) * 128]
        for b in range(blocks):
            out_ref[:, b * 128 : (b + 1) * 128] = stage[b].astype(BF16)

    block = pl.BlockSpec((1, rows_n, 2 * hidden), lambda i: (layer, 0, 0))
    whole = pl.BlockSpec((n_in, lanes), lambda i: (0, 0))
    out_shape = [jax.ShapeDtypeStruct(kept.shape, BF16)]
    out_specs = [block]
    if not last:
        out_shape.append(jax.ShapeDtypeStruct((n_in, lanes), BF16))
        out_specs.append(whole)
    return pl.pallas_call(
        body,
        grid=(1,),
        in_specs=[
            whole,
            pl.BlockSpec(memory_space=pltpu.HBM),
            block,
            pl.BlockSpec(memory_space=pl.ANY),
        ],
        out_specs=out_specs,
        out_shape=out_shape,
        scratch_shapes=[
            pltpu.VMEM((mats, 2, chunks, rows_c, half), BF16),
            pltpu.VMEM((lanes // 128, n_in, 128), F32),
            pltpu.SemaphoreType.DMA((3, 2)),
        ],
        input_output_aliases={3: 0},
        cost_estimate=pl.CostEstimate(
            flops=6 * rows_n * hidden * 2 * half, bytes_accessed=mats * 4 * hidden * half, transcendentals=0
        ),
        name="expert",
    )(rows, weights, fac, kept)


def factor_call(units, pair):
    width, micro, size, lanes = units.shape
    cap = size // PARTS
    rows_n = width * cap
    _, _, hidden, half = pair.shape
    per_half = half // lanes
    blocks = lanes // 128
    step = 4
    n_in = step * width * size

    def body(u_ref, w_ref, rows_ref, fac_ref, stage):
        for m in range(step):
            for b in range(blocks):
                block = u_ref[:, m, :, b * 128 : (b + 1) * 128].astype(F32)
                stage[b, m * width * size : (m + 1) * width * size] = block.reshape(width * size, 128)
        gate = jnp.zeros((step * rows_n, hidden), F32)
        up = jnp.zeros((step * rows_n, hidden), F32)
        for k in range(PARTS):
            part = jnp.concatenate(
                [stage[b, pl.ds(k, step * rows_n, stride=PARTS), :] for b in range(blocks)], axis=1
            ).astype(BF16)
            rows_ref[:, k * lanes : (k + 1) * lanes] = part
            c, j = k // per_half, k % per_half
            gate = gate + dot_t(part, w_ref[0, c, :, j * lanes : (j + 1) * lanes])
            up = up + dot_t(part, w_ref[1, c, :, j * lanes : (j + 1) * lanes])
        sig = jax.nn.sigmoid(gate)
        a = (up * sig * (1.0 + gate * (1.0 - sig))).astype(BF16)
        b = (gate * sig).astype(BF16)
        for m in range(step):
            fac_ref[m, :, :hidden] = a[m * rows_n : (m + 1) * rows_n]
            fac_ref[m, :, hidden:] = b[m * rows_n : (m + 1) * rows_n]

    return pl.pallas_call(
        body,
        grid=(micro // step,),
        in_specs=[
            pl.BlockSpec((width, step, size, lanes), lambda i: (0, i, 0, 0)),
            pl.BlockSpec((2, 2, hidden, half), lambda i: (0, 0, 0, 0)),
        ],
        out_specs=[
            pl.BlockSpec((step * rows_n, PARTS * lanes), lambda i: (i, 0)),
            pl.BlockSpec((step, rows_n, 2 * hidden), lambda i: (i, 0, 0)),
        ],
        out_shape=[
            jax.ShapeDtypeStruct((micro * rows_n, PARTS * lanes), BF16),
            jax.ShapeDtypeStruct((micro, rows_n, 2 * hidden), BF16),
        ],
        scratch_shapes=[pltpu.VMEM((blocks, n_in, 128), F32)],
        cost_estimate=pl.CostEstimate(
            flops=4 * micro * rows_n * hidden * 2 * half,
            bytes_accessed=4 * micro * rows_n * 2 * half,
            transcendentals=micro * rows_n * hidden,
        ),
        name="factors",
    )(units, pair)


def spread(send_ref, g, experts):
    size = g.shape[0] // experts
    for e in range(experts):
        piece = g[e * size : (e + 1) * size].astype(BF16)
        for q in range(GROUP):
            send_ref[e * GROUP + q] = piece


def home_call(layer, experts, back, grad, x, move):
    n_in, lanes = back.shape
    slots = n_in // GROUP
    size = slots // experts
    features = PARTS * lanes

    def body(back_ref, grad_ref, x_ref, move_ref, out_ref, send_ref):
        total = back_ref[...].astype(F32).reshape(experts, GROUP, size, lanes).sum(axis=1)
        total = total.reshape(slots, lanes)
        xf = x_ref[0].astype(F32)
        square = jnp.sum(xf * xf, axis=1, keepdims=True)
        cross = jnp.sum(total * xf, axis=1, keepdims=True)
        row = lax.broadcasted_iota(jnp.int32, (slots, slots), 0) // PARTS
        col = lax.broadcasted_iota(jnp.int32, (slots, slots), 1) // PARTS
        same = (row == col).astype(F32) * (1.0 / features)
        lane = lax.broadcasted_iota(jnp.int32, (slots, 128), 1)
        sums = jnp.where(lane < 64, square, cross)
        means = lax.dot_general(
            same, sums, (((1,), (0,)), ((), ())),
            precision=lax.Precision.HIGHEST, preferred_element_type=F32,
        )
        scale = lax.rsqrt(means[:, :1] + EPS)
        mean = scale * means[:, 64:65]
        grad_new = grad_ref[...].astype(F32) + scale * (total - (xf * scale) * mean)
        moved = dot_n(move_ref[0], grad_new.astype(BF16))
        out_ref[...] = moved.astype(BF16)
        spread(send_ref, moved, experts)

    return pl.pallas_call(
        body,
        grid=(1,),
        in_specs=[
            pl.BlockSpec((n_in, lanes), lambda i: (0, 0)),
            pl.BlockSpec((slots, lanes), lambda i: (0, 0)),
            pl.BlockSpec((1, slots, lanes), lambda i: (layer, 0, 0)),
            pl.BlockSpec((1, slots, slots), lambda i: (layer, 0, 0)),
        ],
        out_specs=[
            pl.BlockSpec((slots, lanes), lambda i: (0, 0)),
            pl.BlockSpec((experts * GROUP, size, lanes), lambda i: (0, 0, 0)),
        ],
        out_shape=[
            jax.ShapeDtypeStruct((slots, lanes), BF16),
            jax.ShapeDtypeStruct((experts * GROUP, size, lanes), BF16),
        ],
        cost_estimate=pl.CostEstimate(flops=10 * n_in * lanes, bytes_accessed=4 * n_in * lanes, transcendentals=0),
        name="home",
    )(back, grad, x, move)


def shards(saved, cotangent, routes, w_gate, w_up, w_down):
    layers = lax.axis_size("pipe")
    width = lax.axis_size("expert")
    dp_index = lax.axis_index("dp")
    experts = width // GROUP
    feat = saved.shape[3]
    half = w_gate.shape[3]
    hidden = w_gate.shape[2]
    tok = saved.shape[2] // MICRO
    cap = tok // experts
    rows_n = width * cap
    lanes = feat // PARTS
    slots = tok * PARTS
    size = cap * PARTS

    z = lax.axis_index("pipe")

    def to_planes(blocks):
        got = blocks
        for d in range(1, layers):
            piece = lax.dynamic_index_in_dim(blocks, (z - d + layers) % layers, 0, keepdims=False)
            piece = lax.ppermute(piece, "pipe", [((p + d) % layers, p) for p in range(layers)])
            got = lax.dynamic_update_index_in_dim(got, piece, (z + d) % layers, 0)
        return got

    place = placing_of(routes[0, 0, :, 0].reshape(MICRO, tok), experts, cap)
    x = saved[0, 0].reshape(MICRO, tok, feat)
    x_slot = jnp.einsum("mst,mtd->msd", place, x, preferred_element_type=F32)
    scale = lax.rsqrt(jnp.mean(x_slot * x_slot, axis=2, keepdims=True) + EPS)
    unit = (x_slot * scale).astype(BF16).reshape(MICRO, experts, size, lanes)
    unit = jnp.transpose(unit, (1, 0, 2, 3))[:, None]
    send = jnp.broadcast_to(unit, (experts, GROUP, MICRO, size, lanes)).reshape(width, MICRO, size, lanes)
    units = lax.all_to_all(send, "expert", split_axis=0, concat_axis=0, tiled=True)

    cut = jnp.stack([w_down[0, 0], w_gate[0, 0], w_up[0, 0]]).reshape(3, layers, hidden // layers, half)
    cut = to_planes(jnp.transpose(cut, (1, 0, 2, 3)))
    weights = {}
    for members in SETS:
        low = min(members)
        mine = cut[low : low + len(members)]
        got = lax.all_gather(mine, ("pipe", "dp"), axis=0).reshape(
            layers, 2, len(members), 3, hidden // layers, half
        )
        for layer in members:
            weights[layer] = (got, layer - low)

    thin = cotangent.shape[1] // PARTS
    extra = jnp.concatenate(
        [
            jnp.repeat(place, PARTS, axis=1),
            cotangent.reshape(MICRO, slots, thin),
            jnp.zeros((MICRO, slots, 128 - tok - thin), BF16),
        ],
        axis=2,
    )
    pack = jnp.concatenate([x_slot.astype(BF16).reshape(MICRO, slots, lanes), extra], axis=2)
    pack = to_planes(pack)
    x_all = pack[:, :, :lanes]
    place_all = pack[:, :, lanes : lanes + tok]
    grad = pack[:, :, lanes + tok : lanes + tok + thin].reshape(layers, tok, PARTS * thin)
    grad = jnp.transpose(grad, (1, 0, 2)).reshape(tok, feat)
    grad = dot_n(place_all[layers - 1, ::PARTS], grad).astype(BF16).reshape(slots, lanes)
    quarter = jnp.arange(slots, dtype=jnp.int32) % PARTS
    move = jnp.einsum("lat,lbt->lab", jnp.roll(place_all, 1, axis=0), place_all, preferred_element_type=F32)
    move = jnp.where(quarter[:, None] == quarter[None, :], move, 0.0).astype(BF16)

    swap = [(0, 1), (1, 0)]
    pair = jnp.stack([w_gate[0, 0], w_up[0, 0]])
    pair_other = lax.ppermute(pair, "dp", swap)
    first = dp_index == 0
    pair = jnp.stack([jnp.where(first, pair, pair_other), jnp.where(first, pair_other, pair)], axis=1)
    unit_rows, fac = factor_call(units, pair)
    fac = lax.all_to_all(fac, "pipe", split_axis=0, concat_axis=0, tiled=True)

    def exchange(block):
        block = block.reshape(width, size, lanes)
        block = lax.all_to_all(block, "expert", split_axis=0, concat_axis=0, tiled=True)
        return block.reshape(width * size, lanes)

    kept = jnp.zeros((layers, rows_n, 2 * hidden), BF16)
    send = jnp.broadcast_to(
        grad.reshape(experts, 1, size, lanes), (experts, GROUP, size, lanes)
    ).reshape(width, size, lanes)
    for layer in range(layers - 1, -1, -1):
        rows = exchange(send)
        got, where = weights[layer]
        if layer == 0:
            (kept,) = expert_call(layer, where, True, rows, got, fac, kept)
            break
        kept, partial = expert_call(layer, where, False, rows, got, fac, kept)
        grad, send = home_call(layer, experts, exchange(partial), grad, x_all, move)

    grads = lax.all_to_all(kept, "pipe", split_axis=0, concat_axis=0, tiled=True)
    grads = grads.reshape(MICRO * rows_n, 2 * hidden)

    def outer(rows):
        return lax.dot_general(
            grads, rows, (((0,), (0,)), ((), ())), preferred_element_type=F32
        ).astype(BF16)

    own = lax.dynamic_slice_in_dim(unit_rows, dp_index * half, half, 1)
    other = lax.dynamic_slice_in_dim(unit_rows, (1 - dp_index) * half, half, 1)
    got = lax.ppermute(outer(other), "dp", swap)
    total = (outer(own).astype(F32) + got.astype(F32)).astype(BF16)
    return total[None, None, :hidden], total[None, None, hidden:]


def solution(mesh):
    in_specs = (
        P(None, "pipe", ("expert", "dp"), None),
        P(("expert", "dp"), "pipe"),
        P(None, "pipe", ("expert", "dp"), None),
        P(None, "pipe", "expert", "dp"),
        P(None, "pipe", "expert", "dp"),
        P(None, "pipe", "expert", "dp"),
    )
    out_specs = (P(None, "pipe", "expert", "dp"), P(None, "pipe", "expert", "dp"))
    return jax.shard_map(shards, mesh=mesh, in_specs=in_specs, out_specs=out_specs, check_vma=False)
```

```python
import jax
import jax.numpy as jnp
from jax import lax
from jax.experimental import pallas as pl
from jax.experimental.pallas import tpu as pltpu
from jax.sharding import PartitionSpec as P


GROUP = 4
MICRO = 8
PARTS = 4
EPS = 1e-06
F32 = jnp.float32
BF16 = jnp.bfloat16
LIMIT = 48 * 1024 * 1024
SETS = ((7, 6), (5, 4, 3), (2, 1, 0))


def dot_t(a, b):
    return lax.dot_general(a, b, (((1,), (1,)), ((), ())), preferred_element_type=F32)


def dot_n(a, b):
    return lax.dot_general(a, b, (((1,), (0,)), ((), ())), preferred_element_type=F32)


def placing_of(route_ids, experts, capacity):
    onehot = (route_ids[..., None] == jnp.arange(experts, dtype=jnp.int32)).astype(jnp.int32)
    ranking = jnp.sum((jnp.cumsum(onehot, axis=1) - onehot) * onehot, axis=2)
    slot_ids = route_ids * capacity + ranking
    positions = jnp.arange(experts * capacity, dtype=jnp.int32)[:, None]
    return (slot_ids[:, None, :] == positions).astype(BF16)


def load(src, where, dst, sem):
    return [
        [pltpu.make_async_copy(src.at[:, c, where, m], dst.at[m, c], sem.at[m, c]) for c in range(2)]
        for m in range(dst.shape[0])
    ]


def expert_call(layer, where, last, rows, weights, fac, kept):
    n_in, lanes = rows.shape
    rows_n = n_in // PARTS
    loaded = where is None
    if loaded:
        _, _, chunks, rows_c, half = weights.shape
    else:
        chunks, _, _, _, rows_c, half = weights.shape
    hidden = chunks * rows_c
    per_half = half // lanes
    mats = 1 if last else 3

    def body(rows_ref, w_ref, fac_ref, _, *refs):
        refs = list(refs)
        kept_ref = refs.pop(0)
        out_ref = None if last else refs.pop(0)
        stage = refs.pop(0)
        if loaded:
            w_vm = w_ref
        else:
            w_vm, sem = refs
            copies = load(w_ref, where, w_vm, sem)
            for pair in copies:
                for copy in pair:
                    copy.start()
        blocks = lanes // 128
        for b in range(blocks):
            stage[b] = rows_ref[:, b * 128 : (b + 1) * 128].astype(F32)
        hidden_grad = jnp.zeros((rows_n, hidden), F32)
        for c in range(2):
            if not loaded:
                copies[0][c].wait()
            for j in range(per_half):
                k = c * per_half + j
                part = jnp.concatenate(
                    [stage[b, pl.ds(k, rows_n, stride=PARTS), :] for b in range(blocks)], axis=1
                ).astype(BF16)
                w = w_vm[0, c, :, :, j * lanes : (j + 1) * lanes].reshape(hidden, lanes)
                hidden_grad = hidden_grad + dot_t(part, w)
        f = fac_ref[0].astype(F32)
        gate_grad = (hidden_grad * f[:, :hidden]).astype(BF16)
        up_grad = (hidden_grad * f[:, hidden:]).astype(BF16)
        kept_ref[0, :, :hidden] = gate_grad
        kept_ref[0, :, hidden:] = up_grad
        if last:
            return
        for c in range(2):
            if not loaded:
                copies[1][c].wait()
                copies[2][c].wait()
            for j in range(per_half):
                k = c * per_half + j
                g = w_vm[1, c, :, :, j * lanes : (j + 1) * lanes].reshape(hidden, lanes)
                u = w_vm[2, c, :, :, j * lanes : (j + 1) * lanes].reshape(hidden, lanes)
                part = dot_n(gate_grad, g) + dot_n(up_grad, u)
                for b in range(blocks):
                    stage[b, pl.ds(k, rows_n, stride=PARTS), :] = part[:, b * 128 : (b + 1) * 128]
        for b in range(blocks):
            out_ref[:, b * 128 : (b + 1) * 128] = stage[b].astype(BF16)

    block = pl.BlockSpec((1, rows_n, 2 * hidden), lambda i: (layer, 0, 0))
    whole = pl.BlockSpec((n_in, lanes), lambda i: (0, 0))
    out_shape = [jax.ShapeDtypeStruct(kept.shape, BF16)]
    out_specs = [block]
    if not last:
        out_shape.append(jax.ShapeDtypeStruct((n_in, lanes), BF16))
        out_specs.append(whole)
    return pl.pallas_call(
        body,
        grid=(1,),
        in_specs=[
            whole,
            pl.BlockSpec(memory_space=pltpu.VMEM if loaded else pltpu.HBM),
            block,
            pl.BlockSpec(memory_space=pl.ANY),
        ],
        out_specs=out_specs,
        out_shape=out_shape,
        scratch_shapes=[pltpu.VMEM((lanes // 128, n_in, 128), F32)]
        + (
            []
            if loaded
            else [pltpu.VMEM((mats, 2, chunks, rows_c, half), BF16), pltpu.SemaphoreType.DMA((mats, 2))]
        ),
        input_output_aliases={3: 0},
        compiler_params=pltpu.CompilerParams(vmem_limit_bytes=LIMIT),
        cost_estimate=pl.CostEstimate(
            flops=6 * rows_n * hidden * 2 * half, bytes_accessed=mats * 4 * hidden * half, transcendentals=0
        ),
        name="expert",
    )(rows, weights, fac, kept)


def factor_call(units, pair):
    width, micro, size, lanes = units.shape
    cap = size // PARTS
    rows_n = width * cap
    _, _, hidden, half = pair.shape
    per_half = half // lanes
    blocks = lanes // 128
    step = 4
    n_in = step * width * size

    def body(u_ref, w_ref, rows_ref, fac_ref, stage):
        for m in range(step):
            for b in range(blocks):
                block = u_ref[:, m, :, b * 128 : (b + 1) * 128].astype(F32)
                stage[b, m * width * size : (m + 1) * width * size] = block.reshape(width * size, 128)
        gate = jnp.zeros((step * rows_n, hidden), F32)
        up = jnp.zeros((step * rows_n, hidden), F32)
        for k in range(PARTS):
            part = jnp.concatenate(
                [stage[b, pl.ds(k, step * rows_n, stride=PARTS), :] for b in range(blocks)], axis=1
            ).astype(BF16)
            rows_ref[:, k * lanes : (k + 1) * lanes] = part
            c, j = k // per_half, k % per_half
            gate = gate + dot_t(part, w_ref[0, c, :, j * lanes : (j + 1) * lanes])
            up = up + dot_t(part, w_ref[1, c, :, j * lanes : (j + 1) * lanes])
        sig = jax.nn.sigmoid(gate)
        a = (up * sig * (1.0 + gate * (1.0 - sig))).astype(BF16)
        b = (gate * sig).astype(BF16)
        for m in range(step):
            fac_ref[m, :, :hidden] = a[m * rows_n : (m + 1) * rows_n]
            fac_ref[m, :, hidden:] = b[m * rows_n : (m + 1) * rows_n]

    return pl.pallas_call(
        body,
        grid=(micro // step,),
        in_specs=[
            pl.BlockSpec((width, step, size, lanes), lambda i: (0, i, 0, 0)),
            pl.BlockSpec((2, 2, hidden, half), lambda i: (0, 0, 0, 0)),
        ],
        out_specs=[
            pl.BlockSpec((step * rows_n, PARTS * lanes), lambda i: (i, 0)),
            pl.BlockSpec((step, rows_n, 2 * hidden), lambda i: (i, 0, 0)),
        ],
        out_shape=[
            jax.ShapeDtypeStruct((micro * rows_n, PARTS * lanes), BF16),
            jax.ShapeDtypeStruct((micro, rows_n, 2 * hidden), BF16),
        ],
        scratch_shapes=[pltpu.VMEM((blocks, n_in, 128), F32)],
        cost_estimate=pl.CostEstimate(
            flops=4 * micro * rows_n * hidden * 2 * half,
            bytes_accessed=4 * micro * rows_n * 2 * half,
            transcendentals=micro * rows_n * hidden,
        ),
        name="factors",
    )(units, pair)


def spread(send_ref, g, experts):
    size = g.shape[0] // experts
    for e in range(experts):
        piece = g[e * size : (e + 1) * size].astype(BF16)
        for q in range(GROUP):
            send_ref[e * GROUP + q] = piece


def home_call(layer, experts, back, grad, x, move, weights, where, mats):
    chunks, _, _, _, rows_c, half = weights.shape
    n_in, lanes = back.shape
    slots = n_in // GROUP
    size = slots // experts
    features = PARTS * lanes

    def body(back_ref, grad_ref, x_ref, move_ref, w_ref, out_ref, send_ref, next_ref, sem):
        copies = load(w_ref, where, next_ref, sem)
        for pair in copies:
            for copy in pair:
                copy.start()
        total = back_ref[...].astype(F32).reshape(experts, GROUP, size, lanes).sum(axis=1)
        total = total.reshape(slots, lanes)
        xf = x_ref[0].astype(F32)
        square = jnp.sum(xf * xf, axis=1, keepdims=True)
        cross = jnp.sum(total * xf, axis=1, keepdims=True)
        row = lax.broadcasted_iota(jnp.int32, (slots, slots), 0) // PARTS
        col = lax.broadcasted_iota(jnp.int32, (slots, slots), 1) // PARTS
        same = (row == col).astype(F32) * (1.0 / features)
        lane = lax.broadcasted_iota(jnp.int32, (slots, 128), 1)
        sums = jnp.where(lane < 64, square, cross)
        means = lax.dot_general(
            same, sums, (((1,), (0,)), ((), ())),
            precision=lax.Precision.HIGHEST, preferred_element_type=F32,
        )
        scale = lax.rsqrt(means[:, :1] + EPS)
        mean = scale * means[:, 64:65]
        grad_new = grad_ref[...].astype(F32) + scale * (total - (xf * scale) * mean)
        moved = dot_n(move_ref[0], grad_new.astype(BF16))
        out_ref[...] = moved.astype(BF16)
        spread(send_ref, moved, experts)
        for pair in copies:
            for copy in pair:
                copy.wait()

    return pl.pallas_call(
        body,
        grid=(1,),
        in_specs=[
            pl.BlockSpec((n_in, lanes), lambda i: (0, 0)),
            pl.BlockSpec((slots, lanes), lambda i: (0, 0)),
            pl.BlockSpec((1, slots, lanes), lambda i: (layer, 0, 0)),
            pl.BlockSpec((1, slots, slots), lambda i: (layer, 0, 0)),
            pl.BlockSpec(memory_space=pltpu.HBM),
        ],
        out_specs=[
            pl.BlockSpec((slots, lanes), lambda i: (0, 0)),
            pl.BlockSpec((experts * GROUP, size, lanes), lambda i: (0, 0, 0)),
            pl.BlockSpec(memory_space=pltpu.VMEM),
        ],
        out_shape=[
            jax.ShapeDtypeStruct((slots, lanes), BF16),
            jax.ShapeDtypeStruct((experts * GROUP, size, lanes), BF16),
            jax.ShapeDtypeStruct((mats, 2, chunks, rows_c, half), BF16),
        ],
        scratch_shapes=[pltpu.SemaphoreType.DMA((mats, 2))],
        compiler_params=pltpu.CompilerParams(vmem_limit_bytes=LIMIT),
        cost_estimate=pl.CostEstimate(flops=10 * n_in * lanes, bytes_accessed=4 * n_in * lanes, transcendentals=0),
        name="home",
    )(back, grad, x, move, weights)


def shards(saved, cotangent, routes, w_gate, w_up, w_down):
    layers = lax.axis_size("pipe")
    width = lax.axis_size("expert")
    dp_index = lax.axis_index("dp")
    experts = width // GROUP
    feat = saved.shape[3]
    half = w_gate.shape[3]
    hidden = w_gate.shape[2]
    tok = saved.shape[2] // MICRO
    cap = tok // experts
    rows_n = width * cap
    lanes = feat // PARTS
    slots = tok * PARTS
    size = cap * PARTS

    z = lax.axis_index("pipe")

    def to_planes(blocks):
        got = blocks
        for d in range(1, layers):
            piece = lax.dynamic_index_in_dim(blocks, (z - d + layers) % layers, 0, keepdims=False)
            piece = lax.ppermute(piece, "pipe", [((p + d) % layers, p) for p in range(layers)])
            got = lax.dynamic_update_index_in_dim(got, piece, (z + d) % layers, 0)
        return got

    place = placing_of(routes[0, 0, :, 0].reshape(MICRO, tok), experts, cap)
    x = saved[0, 0].reshape(MICRO, tok, feat)
    x_slot = jnp.einsum("mst,mtd->msd", place, x, preferred_element_type=F32)
    scale = lax.rsqrt(jnp.mean(x_slot * x_slot, axis=2, keepdims=True) + EPS)
    unit = (x_slot * scale).astype(BF16).reshape(MICRO, experts, size, lanes)
    unit = jnp.transpose(unit, (1, 0, 2, 3))[:, None]
    send = jnp.broadcast_to(unit, (experts, GROUP, MICRO, size, lanes)).reshape(width, MICRO, size, lanes)
    units = lax.all_to_all(send, "expert", split_axis=0, concat_axis=0, tiled=True)

    cut = jnp.stack([w_down[0, 0], w_gate[0, 0], w_up[0, 0]]).reshape(3, layers, hidden // layers, half)
    cut = to_planes(jnp.transpose(cut, (1, 0, 2, 3)))
    weights = {}
    for members in SETS:
        low = min(members)
        mine = cut[low : low + len(members)]
        got = lax.all_gather(mine, ("pipe", "dp"), axis=0)
        got = got.reshape(layers, 2, len(members), 3, hidden // layers, half)
        for layer in members:
            weights[layer] = (got, layer - low)

    thin = cotangent.shape[1] // PARTS
    extra = jnp.concatenate(
        [
            jnp.repeat(place, PARTS, axis=1),
            cotangent.reshape(MICRO, slots, thin),
            jnp.zeros((MICRO, slots, 128 - tok - thin), BF16),
        ],
        axis=2,
    )
    pack = jnp.concatenate([x_slot.astype(BF16).reshape(MICRO, slots, lanes), extra], axis=2)
    pack = to_planes(pack)
    x_all = pack[:, :, :lanes]
    place_all = pack[:, :, lanes : lanes + tok]
    grad = pack[:, :, lanes + tok : lanes + tok + thin].reshape(layers, tok, PARTS * thin)
    grad = jnp.transpose(grad, (1, 0, 2)).reshape(tok, feat)
    grad = dot_n(place_all[layers - 1, ::PARTS], grad).astype(BF16).reshape(slots, lanes)
    quarter = jnp.arange(slots, dtype=jnp.int32) % PARTS
    move = jnp.einsum("lat,lbt->lab", jnp.roll(place_all, 1, axis=0), place_all, preferred_element_type=F32)
    move = jnp.where(quarter[:, None] == quarter[None, :], move, 0.0).astype(BF16)

    swap = [(0, 1), (1, 0)]
    pair = jnp.stack([w_gate[0, 0], w_up[0, 0]])
    pair_other = lax.ppermute(pair, "dp", swap)
    first = dp_index == 0
    pair = jnp.stack([jnp.where(first, pair, pair_other), jnp.where(first, pair_other, pair)], axis=1)
    unit_rows, fac = factor_call(units, pair)
    fac = lax.all_to_all(fac, "pipe", split_axis=0, concat_axis=0, tiled=True)

    def exchange(block):
        block = block.reshape(width, size, lanes)
        block = lax.all_to_all(block, "expert", split_axis=0, concat_axis=0, tiled=True)
        return block.reshape(width * size, lanes)

    kept = jnp.zeros((layers, rows_n, 2 * hidden), BF16)
    send = jnp.broadcast_to(
        grad.reshape(experts, 1, size, lanes), (experts, GROUP, size, lanes)
    ).reshape(width, size, lanes)
    for layer in range(layers - 1, -1, -1):
        rows = exchange(send)
        if layer == 0:
            (kept,) = expert_call(layer, None, True, rows, loaded, fac, kept)
            break
        if layer == layers - 1:
            kept, partial = expert_call(layer, weights[layer][1], False, rows, weights[layer][0], fac, kept)
        else:
            kept, partial = expert_call(layer, None, False, rows, loaded, fac, kept)
        grad, send, loaded = home_call(
            layer, experts, exchange(partial), grad, x_all, move, *weights[layer - 1], 1 if layer == 1 else 3
        )

    grads = lax.all_to_all(kept, "pipe", split_axis=0, concat_axis=0, tiled=True)
    grads = grads.reshape(MICRO * rows_n, 2 * hidden)

    def outer(rows):
        return lax.dot_general(
            grads, rows, (((0,), (0,)), ((), ())), preferred_element_type=F32
        ).astype(BF16)

    own = lax.dynamic_slice_in_dim(unit_rows, dp_index * half, half, 1)
    other = lax.dynamic_slice_in_dim(unit_rows, (1 - dp_index) * half, half, 1)
    got = lax.ppermute(outer(other), "dp", swap)
    total = (outer(own).astype(F32) + got.astype(F32)).astype(BF16)
    return total[None, None, :hidden], total[None, None, hidden:]


def solution(mesh):
    in_specs = (
        P(None, "pipe", ("expert", "dp"), None),
        P(("expert", "dp"), "pipe"),
        P(None, "pipe", ("expert", "dp"), None),
        P(None, "pipe", "expert", "dp"),
        P(None, "pipe", "expert", "dp"),
        P(None, "pipe", "expert", "dp"),
    )
    out_specs = (P(None, "pipe", "expert", "dp"), P(None, "pipe", "expert", "dp"))
    return jax.shard_map(shards, mesh=mesh, in_specs=in_specs, out_specs=out_specs, check_vma=False)
```

```python
import jax
import jax.numpy as jnp
from jax import lax
from jax.experimental import pallas as pl
from jax.experimental.pallas import tpu as pltpu
from jax.sharding import PartitionSpec as P


GROUP = 4
MICRO = 8
PARTS = 4
EPS = 1e-06
F32 = jnp.float32
BF16 = jnp.bfloat16
LIMIT = 48 * 1024 * 1024
SETS = ((7, 6), (5, 4), (3, 2, 1, 0))


def dot_t(a, b):
    return lax.dot_general(a, b, (((1,), (1,)), ((), ())), preferred_element_type=F32)


def dot_n(a, b):
    return lax.dot_general(a, b, (((1,), (0,)), ((), ())), preferred_element_type=F32)


def placing_of(route_ids, experts, capacity):
    onehot = (route_ids[..., None] == jnp.arange(experts, dtype=jnp.int32)).astype(jnp.int32)
    ranking = jnp.sum((jnp.cumsum(onehot, axis=1) - onehot) * onehot, axis=2)
    slot_ids = route_ids * capacity + ranking
    positions = jnp.arange(experts * capacity, dtype=jnp.int32)[:, None]
    return (slot_ids[:, None, :] == positions).astype(BF16)


def load(src, where, dst, sem):
    return [
        [pltpu.make_async_copy(src.at[:, c, where, m], dst.at[m, c], sem.at[m, c]) for c in range(2)]
        for m in range(dst.shape[0])
    ]


def expert_call(layer, where, last, rows, weights, fac, kept):
    n_in, lanes = rows.shape
    rows_n = n_in // PARTS
    loaded = where is None
    if loaded:
        _, _, chunks, rows_c, half = weights.shape
    else:
        chunks, _, _, _, rows_c, half = weights.shape
    hidden = chunks * rows_c
    per_half = half // lanes
    mats = 1 if last else 3

    def body(rows_ref, w_ref, fac_ref, _, *refs):
        refs = list(refs)
        kept_ref = refs.pop(0)
        out_ref = None if last else refs.pop(0)
        stage = refs.pop(0)
        if loaded:
            w_vm = w_ref
        else:
            w_vm, sem = refs
            copies = load(w_ref, where, w_vm, sem)
            for pair in copies:
                for copy in pair:
                    copy.start()
        blocks = lanes // 128
        for b in range(blocks):
            stage[b] = rows_ref[:, b * 128 : (b + 1) * 128].astype(F32)
        hidden_grad = jnp.zeros((rows_n, hidden), F32)
        for c in range(2):
            if not loaded:
                copies[0][c].wait()
            for j in range(per_half):
                k = c * per_half + j
                part = jnp.concatenate(
                    [stage[b, pl.ds(k, rows_n, stride=PARTS), :] for b in range(blocks)], axis=1
                ).astype(BF16)
                w = w_vm[0, c, :, :, j * lanes : (j + 1) * lanes].reshape(hidden, lanes)
                hidden_grad = hidden_grad + dot_t(part, w)
        f = fac_ref[0].astype(F32)
        gate_grad = (hidden_grad * f[:, :hidden]).astype(BF16)
        up_grad = (hidden_grad * f[:, hidden:]).astype(BF16)
        kept_ref[0, :, :hidden] = gate_grad
        kept_ref[0, :, hidden:] = up_grad
        if last:
            return
        for c in range(2):
            if not loaded:
                copies[1][c].wait()
                copies[2][c].wait()
            for j in range(per_half):
                k = c * per_half + j
                g = w_vm[1, c, :, :, j * lanes : (j + 1) * lanes].reshape(hidden, lanes)
                u = w_vm[2, c, :, :, j * lanes : (j + 1) * lanes].reshape(hidden, lanes)
                part = dot_n(gate_grad, g) + dot_n(up_grad, u)
                for b in range(blocks):
                    stage[b, pl.ds(k, rows_n, stride=PARTS), :] = part[:, b * 128 : (b + 1) * 128]
        for b in range(blocks):
            out_ref[:, b * 128 : (b + 1) * 128] = stage[b].astype(BF16)

    block = pl.BlockSpec((1, rows_n, 2 * hidden), lambda i: (layer, 0, 0))
    whole = pl.BlockSpec((n_in, lanes), lambda i: (0, 0))
    out_shape = [jax.ShapeDtypeStruct(kept.shape, BF16)]
    out_specs = [block]
    if not last:
        out_shape.append(jax.ShapeDtypeStruct((n_in, lanes), BF16))
        out_specs.append(whole)
    return pl.pallas_call(
        body,
        grid=(1,),
        in_specs=[
            whole,
            pl.BlockSpec(memory_space=pltpu.VMEM if loaded else pltpu.HBM),
            block,
            pl.BlockSpec(memory_space=pl.ANY),
        ],
        out_specs=out_specs,
        out_shape=out_shape,
        scratch_shapes=[pltpu.VMEM((lanes // 128, n_in, 128), F32)]
        + (
            []
            if loaded
            else [pltpu.VMEM((mats, 2, chunks, rows_c, half), BF16), pltpu.SemaphoreType.DMA((mats, 2))]
        ),
        input_output_aliases={3: 0},
        compiler_params=pltpu.CompilerParams(vmem_limit_bytes=LIMIT // 3 if last else LIMIT),
        cost_estimate=pl.CostEstimate(
            flops=6 * rows_n * hidden * 2 * half, bytes_accessed=mats * 4 * hidden * half, transcendentals=0
        ),
        name="expert",
    )(rows, weights, fac, kept)


def factor_call(units, pair):
    width, micro, size, lanes = units.shape
    cap = size // PARTS
    rows_n = width * cap
    _, _, hidden, half = pair.shape
    per_half = half // lanes
    blocks = lanes // 128
    step = 4
    n_in = step * width * size

    def body(u_ref, w_ref, rows_ref, fac_ref, stage):
        for m in range(step):
            for b in range(blocks):
                block = u_ref[:, m, :, b * 128 : (b + 1) * 128].astype(F32)
                stage[b, m * width * size : (m + 1) * width * size] = block.reshape(width * size, 128)
        gate = jnp.zeros((step * rows_n, hidden), F32)
        up = jnp.zeros((step * rows_n, hidden), F32)
        for k in range(PARTS):
            part = jnp.concatenate(
                [stage[b, pl.ds(k, step * rows_n, stride=PARTS), :] for b in range(blocks)], axis=1
            ).astype(BF16)
            rows_ref[:, k * lanes : (k + 1) * lanes] = part
            c, j = k // per_half, k % per_half
            gate = gate + dot_t(part, w_ref[0, c, :, j * lanes : (j + 1) * lanes])
            up = up + dot_t(part, w_ref[1, c, :, j * lanes : (j + 1) * lanes])
        sig = jax.nn.sigmoid(gate)
        a = (up * sig * (1.0 + gate * (1.0 - sig))).astype(BF16)
        b = (gate * sig).astype(BF16)
        for m in range(step):
            fac_ref[m, :, :hidden] = a[m * rows_n : (m + 1) * rows_n]
            fac_ref[m, :, hidden:] = b[m * rows_n : (m + 1) * rows_n]

    return pl.pallas_call(
        body,
        grid=(micro // step,),
        in_specs=[
            pl.BlockSpec((width, step, size, lanes), lambda i: (0, i, 0, 0)),
            pl.BlockSpec((2, 2, hidden, half), lambda i: (0, 0, 0, 0)),
        ],
        out_specs=[
            pl.BlockSpec((step * rows_n, PARTS * lanes), lambda i: (i, 0)),
            pl.BlockSpec((step, rows_n, 2 * hidden), lambda i: (i, 0, 0)),
        ],
        out_shape=[
            jax.ShapeDtypeStruct((micro * rows_n, PARTS * lanes), BF16),
            jax.ShapeDtypeStruct((micro, rows_n, 2 * hidden), BF16),
        ],
        scratch_shapes=[pltpu.VMEM((blocks, n_in, 128), F32)],
        cost_estimate=pl.CostEstimate(
            flops=4 * micro * rows_n * hidden * 2 * half,
            bytes_accessed=4 * micro * rows_n * 2 * half,
            transcendentals=micro * rows_n * hidden,
        ),
        name="factors",
    )(units, pair)


def spread(send_ref, g, experts):
    size = g.shape[0] // experts
    for e in range(experts):
        piece = g[e * size : (e + 1) * size].astype(BF16)
        for q in range(GROUP):
            send_ref[e * GROUP + q] = piece


def home_call(layer, experts, back, grad, x, move, weights, where, mats):
    chunks, _, _, _, rows_c, half = weights.shape
    n_in, lanes = back.shape
    slots = n_in // GROUP
    size = slots // experts
    features = PARTS * lanes

    def body(back_ref, grad_ref, x_ref, move_ref, w_ref, out_ref, send_ref, next_ref, sem):
        copies = load(w_ref, where, next_ref, sem)
        for pair in copies:
            for copy in pair:
                copy.start()
        total = back_ref[...].astype(F32).reshape(experts, GROUP, size, lanes).sum(axis=1)
        total = total.reshape(slots, lanes)
        xf = x_ref[0].astype(F32)
        square = jnp.sum(xf * xf, axis=1, keepdims=True)
        cross = jnp.sum(total * xf, axis=1, keepdims=True)
        row = lax.broadcasted_iota(jnp.int32, (slots, slots), 0) // PARTS
        col = lax.broadcasted_iota(jnp.int32, (slots, slots), 1) // PARTS
        same = (row == col).astype(F32) * (1.0 / features)
        lane = lax.broadcasted_iota(jnp.int32, (slots, 128), 1)
        sums = jnp.where(lane < 64, square, cross)
        means = lax.dot_general(
            same, sums, (((1,), (0,)), ((), ())),
            precision=lax.Precision.HIGHEST, preferred_element_type=F32,
        )
        scale = lax.rsqrt(means[:, :1] + EPS)
        mean = scale * means[:, 64:65]
        grad_new = grad_ref[...].astype(F32) + scale * (total - (xf * scale) * mean)
        moved = dot_n(move_ref[0], grad_new.astype(BF16))
        out_ref[...] = moved.astype(BF16)
        spread(send_ref, moved, experts)
        for pair in copies:
            for copy in pair:
                copy.wait()

    return pl.pallas_call(
        body,
        grid=(1,),
        in_specs=[
            pl.BlockSpec((n_in, lanes), lambda i: (0, 0)),
            pl.BlockSpec((slots, lanes), lambda i: (0, 0)),
            pl.BlockSpec((1, slots, lanes), lambda i: (layer, 0, 0)),
            pl.BlockSpec((1, slots, slots), lambda i: (layer, 0, 0)),
            pl.BlockSpec(memory_space=pltpu.HBM),
        ],
        out_specs=[
            pl.BlockSpec((slots, lanes), lambda i: (0, 0)),
            pl.BlockSpec((experts * GROUP, size, lanes), lambda i: (0, 0, 0)),
            pl.BlockSpec(memory_space=pltpu.VMEM),
        ],
        out_shape=[
            jax.ShapeDtypeStruct((slots, lanes), BF16),
            jax.ShapeDtypeStruct((experts * GROUP, size, lanes), BF16),
            jax.ShapeDtypeStruct((mats, 2, chunks, rows_c, half), BF16),
        ],
        scratch_shapes=[pltpu.SemaphoreType.DMA((mats, 2))],
        compiler_params=pltpu.CompilerParams(vmem_limit_bytes=LIMIT),
        cost_estimate=pl.CostEstimate(flops=10 * n_in * lanes, bytes_accessed=4 * n_in * lanes, transcendentals=0),
        name="home",
    )(back, grad, x, move, weights)


def shards(saved, cotangent, routes, w_gate, w_up, w_down):
    layers = lax.axis_size("pipe")
    width = lax.axis_size("expert")
    dp_index = lax.axis_index("dp")
    experts = width // GROUP
    feat = saved.shape[3]
    half = w_gate.shape[3]
    hidden = w_gate.shape[2]
    tok = saved.shape[2] // MICRO
    cap = tok // experts
    rows_n = width * cap
    lanes = feat // PARTS
    slots = tok * PARTS
    size = cap * PARTS

    z = lax.axis_index("pipe")

    place = placing_of(routes[0, 0, :, 0].reshape(MICRO, tok), experts, cap)
    x = saved[0, 0].reshape(MICRO, tok, feat)
    x_slot = jnp.einsum("mst,mtd->msd", place, x, preferred_element_type=F32)
    scale = lax.rsqrt(jnp.mean(x_slot * x_slot, axis=2, keepdims=True) + EPS)
    unit = (x_slot * scale).astype(BF16).reshape(MICRO, experts, size, lanes)
    unit = jnp.transpose(unit, (1, 0, 2, 3))[:, None]
    send = jnp.broadcast_to(unit, (experts, GROUP, MICRO, size, lanes)).reshape(width, MICRO, size, lanes)
    units = lax.all_to_all(send, "expert", split_axis=0, concat_axis=0, tiled=True)

    cut = jnp.stack([w_down[0, 0], w_gate[0, 0], w_up[0, 0]]).reshape(3, layers, hidden // layers, half)
    cut = jnp.transpose(cut, (1, 0, 2, 3))
    pieces = [lax.dynamic_index_in_dim(cut, z, 0, keepdims=False)]
    for d in range(1, layers):
        piece = lax.dynamic_index_in_dim(cut, (z - d + layers) % layers, 0, keepdims=False)
        pieces.append(lax.ppermute(piece, "pipe", [((p + d) % layers, p) for p in range(layers)]))

    def of_layer(layer):
        out = pieces[0]
        for d in range(1, layers):
            out = jnp.where((z + d) % layers == layer, pieces[d], out)
        return out

    weights = {}
    for members in SETS:
        low = min(members)
        mine = jnp.stack([of_layer(low + i) for i in range(len(members))])
        got = lax.all_gather(mine, ("pipe", "dp"), axis=0)
        got = got.reshape(layers, 2, len(members), 3, hidden // layers, half)
        for layer in members:
            weights[layer] = (got, layer - low)

    thin = cotangent.shape[1] // PARTS
    extra = jnp.concatenate(
        [
            jnp.repeat(place, PARTS, axis=1),
            cotangent.reshape(MICRO, slots, thin),
            jnp.zeros((MICRO, slots, 128 - tok - thin), BF16),
        ],
        axis=2,
    )
    pack = jnp.concatenate([x_slot.astype(BF16).reshape(MICRO, slots, lanes), extra], axis=2)
    pack = lax.all_to_all(pack, "pipe", split_axis=0, concat_axis=0, tiled=True)
    x_all = pack[:, :, :lanes]
    place_all = pack[:, :, lanes : lanes + tok]
    grad = pack[:, :, lanes + tok : lanes + tok + thin].reshape(layers, tok, PARTS * thin)
    grad = jnp.transpose(grad, (1, 0, 2)).reshape(tok, feat)
    grad = dot_n(place_all[layers - 1, ::PARTS], grad).astype(BF16).reshape(slots, lanes)
    quarter = jnp.arange(slots, dtype=jnp.int32) % PARTS
    move = jnp.einsum("lat,lbt->lab", jnp.roll(place_all, 1, axis=0), place_all, preferred_element_type=F32)
    move = jnp.where(quarter[:, None] == quarter[None, :], move, 0.0).astype(BF16)

    swap = [(0, 1), (1, 0)]
    pair = jnp.stack([w_gate[0, 0], w_up[0, 0]])
    pair_other = lax.ppermute(pair, "dp", swap)
    first = dp_index == 0
    pair = jnp.stack([jnp.where(first, pair, pair_other), jnp.where(first, pair_other, pair)], axis=1)
    unit_rows, fac = factor_call(units, pair)
    fac = lax.all_to_all(fac, "pipe", split_axis=0, concat_axis=0, tiled=True)

    def exchange(block):
        block = block.reshape(width, size, lanes)
        block = lax.all_to_all(block, "expert", split_axis=0, concat_axis=0, tiled=True)
        return block.reshape(width * size, lanes)

    kept = jnp.zeros((layers, rows_n, 2 * hidden), BF16)
    send = jnp.broadcast_to(
        grad.reshape(experts, 1, size, lanes), (experts, GROUP, size, lanes)
    ).reshape(width, size, lanes)
    for layer in range(layers - 1, -1, -1):
        rows = exchange(send)
        if layer == 0:
            (kept,) = expert_call(layer, None, True, rows, loaded, fac, kept)
            break
        if layer == layers - 1:
            kept, partial = expert_call(layer, weights[layer][1], False, rows, weights[layer][0], fac, kept)
        else:
            kept, partial = expert_call(layer, None, False, rows, loaded, fac, kept)
        grad, send, loaded = home_call(
            layer, experts, exchange(partial), grad, x_all, move, *weights[layer - 1], 1 if layer == 1 else 3
        )

    grads = lax.all_to_all(kept, "pipe", split_axis=0, concat_axis=0, tiled=True)
    grads = grads.reshape(MICRO * rows_n, 2 * hidden)

    def outer(rows):
        return lax.dot_general(
            grads, rows, (((0,), (0,)), ((), ())), preferred_element_type=F32
        ).astype(BF16)

    own = lax.dynamic_slice_in_dim(unit_rows, dp_index * half, half, 1)
    other = lax.dynamic_slice_in_dim(unit_rows, (1 - dp_index) * half, half, 1)
    got = lax.ppermute(outer(other), "dp", swap)
    total = (outer(own).astype(F32) + got.astype(F32)).astype(BF16)
    return total[None, None, :hidden], total[None, None, hidden:]


def solution(mesh):
    in_specs = (
        P(None, "pipe", ("expert", "dp"), None),
        P(("expert", "dp"), "pipe"),
        P(None, "pipe", ("expert", "dp"), None),
        P(None, "pipe", "expert", "dp"),
        P(None, "pipe", "expert", "dp"),
        P(None, "pipe", "expert", "dp"),
    )
    out_specs = (P(None, "pipe", "expert", "dp"), P(None, "pipe", "expert", "dp"))
    return jax.shard_map(shards, mesh=mesh, in_specs=in_specs, out_specs=out_specs, check_vma=False)
```
